32 devices in a mesh: row: 8 (over z, y), col: 4 (over x, core).
Axes of the slice: x: 2, y: 2, z: 4, core: 2. Of those that a mesh axis runs over, the one named last changes fastest.
Arguments:
- factor: float32 [2, 1024, 1024], P(None, 'row', 'col'), may hold values from -0.125 to 0.125
- lower_inverse: float32 [2, 512, 1024], P(None, None, 'row'), may hold values from -1 to 2
- upper_inverse: float32 [2, 512, 1024], P(None, None, 'row'), may hold values from -1 to 2
- krylov_block: float32 [2, 16, 1024], P(None, None, 'row'), may hold values from -6 to 6
- basis: float32 [2, 64, 1024], P(None, None, 'row'), may hold values from -0.125 to 0.125
Outputs:
- projected: float32 [2, 16, 1024], P(None, None, 'row')
- coefficients: float32 [2, 64, 16], replicated
The draws below stay inside these ranges and needn't reach their ends.
All inputs are finite; a program needn't handle non-finite values.
Results may differ from the reference program's by a relative error of at most 0.00012.
Values sent between devices are 32-bit elements; how exact they have to be, the bound alone decides.
A program may use at most 64 MiB of HBM per device.

```python
import jax
import jax.numpy as jnp
from jax import lax

TILE = 512
NRHS = 16
NB = 64
KT = 2
N = 1024


def tile_inverse(key):
    cols = jnp.arange(N) % TILE
    ident = (jnp.arange(TILE)[:, None] == cols[None, :]).astype(jnp.float32)
    noise = jax.random.normal(key, (2, TILE, N), jnp.float32) * (0.3 / jnp.sqrt(jnp.float32(TILE)))
    noise = jnp.clip(noise, -0.2, 0.2)
    return jnp.stack([ident + noise[0], noise[1]])


def draw_lower_inverse(key, part):
    return tile_inverse(jax.random.fold_in(key, 101))


def draw_upper_inverse(key, part):
    return tile_inverse(jax.random.fold_in(key, 202))


def steps_of(rng, shape, split, least, top_value):
    def one(dim, shards_of):
        heights = jax.random.uniform(jax.random.fold_in(jax.random.fold_in(rng, 6), dim), (shards_of,), jnp.float32, least / len(split), top_value / len(split))
        return jnp.repeat(jnp.exp(heights), shape[dim] // shards_of).reshape((-1,) + (1,) * (len(shape) - dim - 1))

    factor_of = one(*split[0])
    for cut in split[1:]:
        factor_of = factor_of * one(*cut)
    return factor_of


def gaussian(stream_key, dims, scale, bound, cuts=(), kind=jnp.bfloat16):
    loudness = steps_of(stream_key, dims, cuts, -0.22, 0.18) if cuts else 1.0
    values = jax.random.normal(stream_key, dims, jnp.float32) * scale * loudness
    return jnp.minimum(jnp.maximum(values, -bound), bound).astype(kind)


def setup_inputs(seed: int = 0) -> dict:
    key_of = jax.random.split(jax.random.key(seed), 6)
    factor = gaussian(key_of[0], (2, N, N), (2 * N) ** -0.5, 0.125, ((1, 8), (2, 4)), jnp.float32)
    lower_inverse = draw_lower_inverse(jax.random.fold_in(key_of[5], 71), 0)
    upper_inverse = draw_upper_inverse(jax.random.fold_in(key_of[5], 71), 0)
    krylov_block = gaussian(key_of[3], (2, NRHS, N), 1.0, 6.0, ((2, 8),), jnp.float32)
    basis = gaussian(key_of[4], (2, NB, N), (2 * N) ** -0.5, 0.125, ((2, 8),), jnp.float32)
    return {"factor": factor, "lower_inverse": lower_inverse, "upper_inverse": upper_inverse, "krylov_block": krylov_block, "basis": basis}


def real_dot(left, right):
    return jnp.dot(left, right, preferred_element_type=jnp.float32, precision=lax.Precision.HIGHEST)


def apply_tile(matrix, vectors):
    real_part = real_dot(vectors[0], matrix[0].T) - real_dot(vectors[1], matrix[1].T)
    imag_part = real_dot(vectors[0], matrix[1].T) + real_dot(vectors[1], matrix[0].T)
    return jnp.stack([real_part, imag_part])


def herm_dot(basis_part, vectors):
    real_part = real_dot(basis_part[0], vectors[0].T) + real_dot(basis_part[1], vectors[1].T)
    imag_part = real_dot(basis_part[0], vectors[1].T) - real_dot(basis_part[1], vectors[0].T)
    return jnp.stack([real_part, imag_part])


def combine(basis_part, coeffs):
    real_part = real_dot(coeffs[0].T, basis_part[0]) - real_dot(coeffs[1].T, basis_part[1])
    imag_part = real_dot(coeffs[0].T, basis_part[1]) + real_dot(coeffs[1].T, basis_part[0])
    return jnp.stack([real_part, imag_part])


def sweep(factor, inverse, source, backward):
    start = jnp.zeros(source.shape, jnp.float32)

    def step(index, current):
        k = (KT - 1 - index) if backward else index
        k = jnp.asarray(k).astype(jnp.int32)
        rows = lax.dynamic_slice_in_dim(factor, k * TILE, TILE, 1)
        partial_value = apply_tile(rows, current)
        given = lax.dynamic_slice_in_dim(source, k * TILE, TILE, 2)
        inv = lax.dynamic_slice_in_dim(inverse, k * TILE, TILE, 2)
        piece = apply_tile(inv, given - partial_value)
        return lax.dynamic_update_slice_in_dim(current, piece, k * TILE, 2)

    return lax.fori_loop(0, KT, step, start)


def reference(factor, lower_inverse, upper_inverse, krylov_block, basis):
    solved = sweep(factor, lower_inverse, krylov_block, False)
    solution = sweep(factor, upper_inverse, solved, True)
    first = herm_dot(basis, solution)
    middle = solution - combine(basis, first)
    second = herm_dot(basis, middle)
    projected = middle - combine(basis, second)
    return projected, first + second
```

```python
import functools

import jax
import jax.numpy as jnp
from jax import lax
from jax.experimental import pallas as pl
from jax.experimental.pallas import tpu as pltpu
from jax.sharding import PartitionSpec as P

MESH = pl.DeviceIdType.MESH
F32 = jnp.float32
BF16 = jnp.bfloat16


def split(value):
    high = value.astype(BF16)
    low = (value - high.astype(F32)).astype(BF16)
    return high, low


def dot_nt(left, right):
    return lax.dot_general(left, right, (((1,), (1,)), ((), ())), preferred_element_type=F32)


def dot_nn(left, right):
    return lax.dot_general(left, right, (((1,), (0,)), ((), ())), preferred_element_type=F32)


def product(left, high, low, dot):
    rows = left.shape[0]
    left_high, left_low = split(left)
    both = dot(jnp.concatenate([left_high, left_low], 0), high)
    return both[:rows] + (both[rows:] + dot(left_high, low))


def complex_left(pieces, nvec):
    re = [x[:nvec] for x in pieces]
    im = [x[nvec:] for x in pieces]
    top = jnp.concatenate(re + [-x for x in im], 1)
    bottom = jnp.concatenate(im + re, 1)
    return jnp.concatenate([top, bottom], 0)


def kernel(
    R, C, factor, lower, upper, krylov, basis, projected, coefficients,
    inv_hi, inv_lo, fac_hi, fac_lo, bas_hi, bas_lo,
    psend, precv, ybuf, xbuf, bcast, vbuf, vrecv, fsend, frecv, gacc, grecv,
    psend_sem, precv_sem, bsend_sem, brecv_sem, vsend_sem, vrecv_sem, xsend_sem, xrecv_sem,
    fsend_sem, frecv_sem, gsend_sem, grecv_sem,
):
    tile, rows = lower.shape[1], lower.shape[2]
    width = factor.shape[2]
    nvec = krylov.shape[1]
    nb = basis.shape[1]
    share = tile // rows
    per = tile // width
    pieces = width // rows
    steps = R.bit_length() - 1
    r = lax.axis_index("row")
    c = lax.axis_index("col")
    t, p = r // share, r % share
    j, h = c // per, c % per
    solver = j == t

    barrier = pltpu.get_barrier_semaphore()

    def greet_row(i, carry):
        pl.semaphore_signal(barrier, inc=1, device_id=((r + 1 + i) % R, c), device_id_type=MESH)
        return carry

    def greet_col(i, carry):
        pl.semaphore_signal(barrier, inc=1, device_id=(r, (c + 1 + i) % C), device_id_type=MESH)
        return carry

    lax.fori_loop(0, R - 1, greet_row, 0)
    lax.fori_loop(0, C - 1, greet_col, 0)

    def prepare(ref, slot):
        high, low = split(jnp.concatenate([ref[0], ref[1]], 1))
        inv_hi[slot] = high
        inv_lo[slot] = low

    @pl.when(solver)
    def _():
        prepare(lower, 0)

    @pl.when(jnp.logical_not(solver))
    def _():
        high, low = split(jnp.concatenate([factor[0], factor[1]], 1))
        fac_hi[...] = high
        fac_lo[...] = low

    def prepare_basis():
        top = jnp.concatenate([basis[0], basis[1]], 1)
        bottom = jnp.concatenate([-basis[1], basis[0]], 1)
        high, low = split(jnp.concatenate([top, bottom], 0))
        bas_hi[...] = high
        bas_lo[...] = low
        gacc[0] = product(top, high, low, dot_nt)

    def remote(src, dst, send, recv, dest):
        return pltpu.make_async_remote_copy(
            src_ref=src, dst_ref=dst, send_sem=send, recv_sem=recv, device_id=dest, device_id_type=MESH
        )

    def gram_copy(i):
        other = r + (1 << i) * (1 - 2 * ((r // (1 << i)) % 2))
        return remote(gacc.at[i], grecv.at[i], gsend_sem.at[i], grecv_sem.at[i], (other, c))

    def gram_all():
        for i in range(steps):
            copy = gram_copy(i)
            copy.start()
            copy.wait_recv()
            gacc[i + 1] = gacc[i] + grecv[i]

    def part_copy(sweep, d):
        q = (p + d) % share
        return remote(
            psend.at[sweep, q], precv.at[sweep, p], psend_sem.at[sweep, q], precv_sem.at[sweep, p], (t * share + q, c)
        )

    def part_arrival(sweep, d):
        q = (p + d) % share
        return remote(
            psend.at[sweep, q], precv.at[sweep, q], psend_sem.at[sweep, q], precv_sem.at[sweep, q], (t * share + q, c)
        ), q

    def v_copy(hh):
        return remote(vbuf, vrecv.at[c], vsend_sem.at[hh], vrecv_sem.at[c], (r, t * per + hh))

    def v_sum(first_col, last_col, value):
        def body(cc, total):
            remote(vbuf, vrecv.at[cc], vsend_sem.at[0], vrecv_sem.at[cc], (r, cc)).wait_recv()
            return total - vrecv[cc]

        return lax.fori_loop(first_col, last_col, body, value)

    def solve(sweep, g):
        out = product(complex_left([g], nvec), inv_hi[sweep], inv_lo[sweep], dot_nt)
        for q in range(share):
            psend[sweep, q] = out[:, q * rows:(q + 1) * rows]
        for d in range(1, share):
            part_copy(sweep, d).start()
        total = psend[sweep, p]
        for d in range(1, share):
            arrival, q = part_arrival(sweep, d)
            arrival.wait_recv()
            total = total + precv[sweep, q]
        return total

    def b_copy(buf, rr):
        return remote(buf, bcast.at[p % pieces], bsend_sem.at[rr], brecv_sem.at[p % pieces], (rr, c))

    def each(first_index, last_index, act):
        def body(i, carry):
            act(i)
            return carry

        lax.fori_loop(first_index, last_index, body, 0)

    def x_copy(tt):
        cc = tt * per + h
        return remote(xbuf, xbuf, xsend_sem.at[tt], xrecv_sem.at[0], (r, cc))

    speaks = p // pieces == h

    @pl.when(jnp.logical_and(solver, t > 0))
    def _():
        prepare(upper, 1)

    @pl.when(j > 0)
    def _():
        prepare_basis()

    pl.semaphore_wait(barrier, R - 1 + C - 1)

    @pl.when(j > 0)
    def _():
        gram_all()

    @pl.when(solver)
    def _():
        b = jnp.concatenate([krylov[0], krylov[1]], 0)
        ybuf[...] = solve(0, v_sum(0, t * per, b))

        @pl.when(speaks)
        def _():
            each((t + 1) * share, R, lambda rr: b_copy(ybuf, rr).start())

        @pl.when(t == 0)
        def _():
            prepare(upper, 1)

    @pl.when(jnp.logical_not(solver))
    def _():
        got = []
        for i in range(pieces):
            remote(ybuf, bcast.at[i], bsend_sem.at[0], brecv_sem.at[i], (r, t * per)).wait_recv()
            got.append(bcast[i])
        vbuf[...] = product(complex_left(got, nvec), fac_hi[...], fac_lo[...], dot_nt)
        for hh in range(per):
            v_copy(hh).start()

    @pl.when(j == 0)
    def _():
        prepare_basis()
        gram_all()

    @pl.when(solver)
    def _():
        xbuf[...] = solve(1, v_sum((t + 1) * per, C, ybuf[...]))

        @pl.when(speaks)
        def _():
            each(0, t * share, lambda rr: b_copy(xbuf, rr).start())

        each(0, t, lambda tt: x_copy(tt).start())
        each(t + 1, C // per, lambda tt: x_copy(tt).start())

    @pl.when(jnp.logical_not(solver))
    def _():
        remote(ybuf, xbuf, xsend_sem.at[0], xrecv_sem.at[0], (r, t * per)).wait_recv()

    x = xbuf[...]
    wide = jnp.concatenate([x[:nvec], x[nvec:]], 1)
    fsend[...] = product(wide, bas_hi[...], bas_lo[...], dot_nt)

    def f_copy(d):
        return remote(fsend, frecv.at[r], fsend_sem.at[d], frecv_sem.at[r], ((r + d) % R, c))

    each(1, R, lambda d: f_copy(d).start())
    frecv[r] = fsend[...]

    def f_wait(d):
        q = (r + d) % R
        remote(fsend, frecv.at[q], fsend_sem.at[d], frecv_sem.at[q], (q, c)).wait_recv()

    each(1, R, f_wait)
    first = frecv[0]
    for i in range(1, R):
        first = first + frecv[i]
    top = gacc[steps]
    gram = jnp.concatenate([top, jnp.concatenate([-top[:, nb:], top[:, :nb]], 1)], 0)
    gram_hi, gram_lo = split(gram)
    second = first - product(first, gram_hi, gram_lo, dot_nt)
    coeffs = first + second
    result = wide - product(coeffs, bas_hi[...], bas_lo[...], dot_nn)
    projected[0] = result[:, :rows]
    projected[1] = result[:, rows:]
    turned = coeffs.T
    coefficients[0] = turned[:nb]
    coefficients[1] = turned[nb:]

    each(1, R, lambda d: f_copy(d).wait_send())
    for i in range(steps):
        gram_copy(i).wait_send()

    @pl.when(solver)
    def _():
        for sweep in range(2):
            for d in range(1, share):
                part_copy(sweep, d).wait_send()

        @pl.when(speaks)
        def _():
            each((t + 1) * share, R, lambda rr: b_copy(ybuf, rr).wait_send())
            each(0, t * share, lambda rr: b_copy(xbuf, rr).wait_send())

        each(0, t, lambda tt: x_copy(tt).wait_send())
        each(t + 1, C // per, lambda tt: x_copy(tt).wait_send())

    @pl.when(jnp.logical_not(solver))
    def _():
        for hh in range(per):
            v_copy(hh).wait_send()


def local(R, C, factor, lower, upper, krylov, basis):
    tile, rows = lower.shape[1], lower.shape[2]
    width = factor.shape[2]
    nvec, nb = krylov.shape[1], basis.shape[1]
    share, per, pieces = tile // rows, tile // width, width // rows
    steps = R.bit_length() - 1
    dma = pltpu.SemaphoreType.DMA
    vmem = pl.BlockSpec(memory_space=pltpu.VMEM)
    block = (2 * nvec, rows)
    return pl.pallas_call(
        functools.partial(kernel, R, C),
        out_shape=(
            jax.ShapeDtypeStruct(krylov.shape, F32),
            jax.ShapeDtypeStruct((2, nb, nvec), F32),
        ),
        in_specs=[vmem] * 5,
        out_specs=(vmem, vmem),
        scratch_shapes=[
            pltpu.VMEM((2, tile, 2 * rows), BF16),
            pltpu.VMEM((2, tile, 2 * rows), BF16),
            pltpu.VMEM((rows, 2 * width), BF16),
            pltpu.VMEM((rows, 2 * width), BF16),
            pltpu.VMEM((2 * nb, 2 * rows), BF16),
            pltpu.VMEM((2 * nb, 2 * rows), BF16),
            pltpu.VMEM((2, share) + block, F32),
            pltpu.VMEM((2, share) + block, F32),
            pltpu.VMEM(block, F32),
            pltpu.VMEM(block, F32),
            pltpu.VMEM((pieces,) + block, F32),
            pltpu.VMEM(block, F32),
            pltpu.VMEM((C,) + block, F32),
            pltpu.VMEM((nvec, 2 * nb), F32),
            pltpu.VMEM((R, nvec, 2 * nb), F32),
            pltpu.VMEM((steps + 1, nb, 2 * nb), F32),
            pltpu.VMEM((steps, nb, 2 * nb), F32),
            dma((2, share)),
            dma((2, share)),
            dma((R,)),
            dma((pieces,)),
            dma((per,)),
            dma((C,)),
            dma((C // per,)),
            dma((1,)),
            dma((R,)),
            dma((R,)),
            dma((steps,)),
            dma((steps,)),
        ],
        compiler_params=pltpu.CompilerParams(collective_id=0, has_side_effects=True),
        name="krylov_step",
    )(factor, lower, upper, krylov, basis)


def solution(mesh):
    in_specs = (
        P(None, "row", "col"),
        P(None, None, "row"),
        P(None, None, "row"),
        P(None, None, "row"),
        P(None, None, "row"),
    )
    out_specs = (P(None, None, "row"), P())
    body = functools.partial(local, mesh.shape["row"], mesh.shape["col"])
    return jax.shard_map(body, mesh=mesh, in_specs=in_specs, out_specs=out_specs, check_vma=False)
```

```python
import functools

import jax
import jax.numpy as jnp
from jax import lax
from jax.experimental import pallas as pl
from jax.experimental.pallas import tpu as pltpu
from jax.sharding import PartitionSpec as P

MESH = pl.DeviceIdType.MESH
F32 = jnp.float32
BF16 = jnp.bfloat16


def split(value):
    high = value.astype(BF16)
    low = (value - high.astype(F32)).astype(BF16)
    return high, low


def dot_nt(left, right):
    return lax.dot_general(left, right, (((1,), (1,)), ((), ())), preferred_element_type=F32)


def dot_nn(left, right):
    return lax.dot_general(left, right, (((1,), (0,)), ((), ())), preferred_element_type=F32)


def product(left, high, low, dot):
    rows = left.shape[0]
    left_high, left_low = split(left)
    both = dot(jnp.concatenate([left_high, left_low], 0), high)
    return both[:rows] + (both[rows:] + dot(left_high, low))


def complex_left(pieces, nvec):
    re = [x[:nvec] for x in pieces]
    im = [x[nvec:] for x in pieces]
    top = jnp.concatenate(re + [-x for x in im], 1)
    bottom = jnp.concatenate(im + re, 1)
    return jnp.concatenate([top, bottom], 0)


def kernel(
    R, C, factor, lower, upper, krylov, basis, projected, coefficients,
    inv_hi, inv_lo, fac_hi, fac_lo, bas_hi, bas_lo,
    end_hi, end_lo, lead_hi, lead_lo, gather,
    psend, precv, ybuf, xbuf, bcast, vbuf, vrecv, fsend, frecv, gacc, grecv,
    psend_sem, precv_sem, bsend_sem, brecv_sem, vsend_sem, vrecv_sem, xsend_sem, xrecv_sem,
    fsend_sem, frecv_sem, gsend_sem, grecv_sem, tsend_sem, trecv_sem, ysend_sem, yrecv_sem,
):
    tile, rows = lower.shape[1], lower.shape[2]
    width = factor.shape[2]
    nvec = krylov.shape[1]
    nb = basis.shape[1]
    share = tile // rows
    per = tile // width
    pieces = width // rows
    steps = R.bit_length() - 1
    r = lax.axis_index("row")
    c = lax.axis_index("col")
    t, p = r // share, r % share
    j, h = c // per, c % per
    solver = j == t

    barrier = pltpu.get_barrier_semaphore()

    def greet_row(i, carry):
        pl.semaphore_signal(barrier, inc=1, device_id=((r + 1 + i) % R, c), device_id_type=MESH)
        return carry

    def greet_col(i, carry):
        pl.semaphore_signal(barrier, inc=1, device_id=(r, (c + 1 + i) % C), device_id_type=MESH)
        return carry

    lax.fori_loop(0, R - 1, greet_row, 0)
    lax.fori_loop(0, C - 1, greet_col, 0)

    def prepare(ref, slot):
        high, low = split(jnp.concatenate([ref[0], ref[1]], 1))
        inv_hi[slot] = high
        inv_lo[slot] = low

    @pl.when(solver)
    def _():
        prepare(lower, 0)

    @pl.when(jnp.logical_not(solver))
    def _():
        high, low = split(jnp.concatenate([factor[0], factor[1]], 1))
        fac_hi[...] = high
        fac_lo[...] = low

    def prepare_basis():
        top = jnp.concatenate([basis[0], basis[1]], 1)
        bottom = jnp.concatenate([-basis[1], basis[0]], 1)
        high, low = split(jnp.concatenate([top, bottom], 0))
        bas_hi[...] = high
        bas_lo[...] = low
        gacc[0] = product(top, high, low, dot_nt)

    def remote(src, dst, send, recv, dest):
        return pltpu.make_async_remote_copy(
            src_ref=src, dst_ref=dst, send_sem=send, recv_sem=recv, device_id=dest, device_id_type=MESH
        )

    def each(first_index, last_index, act):
        def body(i, carry):
            act(i)
            return carry

        lax.fori_loop(first_index, last_index, body, 0)

    def gram_copy(i):
        other = r + (1 << i) * (1 - 2 * ((r // (1 << i)) % 2))
        return remote(gacc.at[i], grecv.at[i], gsend_sem.at[i], grecv_sem.at[i], (other, c))

    def gram_all():
        for i in range(steps):
            copy = gram_copy(i)
            copy.start()
            copy.wait_recv()
            gacc[i + 1] = gacc[i] + grecv[i]
        top = gacc[steps]
        gram = jnp.concatenate([top, jnp.concatenate([-top[:, nb:], top[:, :nb]], 1)], 0)
        row_id = lax.broadcasted_iota(jnp.int32, gram.shape, 0)
        col_id = lax.broadcasted_iota(jnp.int32, gram.shape, 1)
        twice = jnp.where(row_id == col_id, 2.0, 0.0) - gram
        spread = product(twice, bas_hi[...], bas_lo[...], dot_nn)
        high, low = split(jnp.concatenate([twice, spread], 1))
        end_hi[...] = high
        end_lo[...] = low

    def t_copy(d):
        q = (p + d) % share
        return remote(basis, gather.at[p], tsend_sem.at[d], trecv_sem.at[p], (t * share + q, c))

    def lead_send():
        for d in range(1, share):
            t_copy(d).start()
        gather[p] = basis[...]

    def lead_all():
        for d in range(1, share):
            q = (p + d) % share
            remote(basis, gather.at[q], tsend_sem.at[d], trecv_sem.at[q], (t * share + q, c)).wait_recv()
        left = jnp.concatenate(
            [jnp.concatenate([gather[q, i] for q in range(share)], 1) for i in range(2)], 0
        )
        out = product(left, inv_hi[1], inv_lo[1], dot_nn)
        one = out[:nb, :rows] + out[nb:, rows:]
        two = out[nb:, :rows] - out[:nb, rows:]
        whole = jnp.concatenate([jnp.concatenate([one, two], 1), jnp.concatenate([-two, one], 1)], 0)
        high, low = split(whole)
        lead_hi[...] = high
        lead_lo[...] = low

    def side_work():
        @pl.when(t == 0)
        def _():
            lead_send()

        gram_all()

        @pl.when(t == 0)
        def _():
            lead_all()

    def part_copy(sweep, d):
        q = (p + d) % share
        return remote(
            psend.at[sweep, q], precv.at[sweep, p], psend_sem.at[sweep, q], precv_sem.at[sweep, p], (t * share + q, c)
        )

    def part_arrival(sweep, d):
        q = (p + d) % share
        return remote(
            psend.at[sweep, q], precv.at[sweep, q], psend_sem.at[sweep, q], precv_sem.at[sweep, q], (t * share + q, c)
        ), q

    def v_copy(cc):
        return remote(vbuf, vrecv.at[c], vsend_sem.at[cc], vrecv_sem.at[c], (r, cc))

    def v_each(act):
        @pl.when(t > 0)
        def _():
            for hh in range(per):
                act(v_copy(t * per + hh))

        @pl.when(t == 0)
        def _():
            each(1, C, lambda d: act(v_copy((c + d) % C)))

    def v_sum(first_col, last_col, value):
        def body(cc, total):
            @pl.when(cc != c)
            def _():
                remote(vbuf, vrecv.at[cc], vsend_sem.at[0], vrecv_sem.at[cc], (r, cc)).wait_recv()

            return total - vrecv[cc]

        return lax.fori_loop(first_col, last_col, body, value)

    def f_copy(d):
        return remote(fsend, frecv.at[r], fsend_sem.at[d], frecv_sem.at[r], ((r + d) % R, c))

    def send_first(value, high, low):
        wide_value = jnp.concatenate([value[:nvec], value[nvec:]], 1)
        fsend[...] = product(wide_value, high, low, dot_nt)
        each(1, R, lambda d: f_copy(d).start())

    def solve(sweep, g):
        out = product(complex_left([g], nvec), inv_hi[sweep], inv_lo[sweep], dot_nt)
        for q in range(share):
            psend[sweep, q] = out[:, q * rows:(q + 1) * rows]
        for d in range(1, share):
            part_copy(sweep, d).start()
        total = psend[sweep, p]
        for d in range(1, share):
            arrival, q = part_arrival(sweep, d)
            arrival.wait_recv()
            total = total + precv[sweep, q]
        return total

    def b_copy(buf, rr):
        return remote(buf, bcast.at[p % pieces], bsend_sem.at[rr], brecv_sem.at[p % pieces], (rr, c))

    def x_copy(tt):
        cc = tt * per + h
        return remote(xbuf, xbuf, xsend_sem.at[tt], xrecv_sem.at[0], (r, cc))

    def y_copy(tt):
        return remote(ybuf, ybuf, ysend_sem.at[tt], yrecv_sem.at[0], (r, tt * per + h))

    speaks = p // pieces == h

    @pl.when(solver != (t == 0))
    def _():
        prepare(upper, 1)

    @pl.when(j > 0)
    def _():
        prepare_basis()

    pl.semaphore_wait(barrier, R - 1 + C - 1)

    @pl.when(j > 0)
    def _():
        side_work()

    @pl.when(solver)
    def _():
        b = jnp.concatenate([krylov[0], krylov[1]], 0)
        ybuf[...] = solve(0, v_sum(0, t * per, b))

        @pl.when(speaks)
        def _():
            each((t + 1) * share, R, lambda rr: b_copy(ybuf, rr).start())

        @pl.when(t == 0)
        def _():
            each(1, C // per, lambda tt: y_copy(tt).start())
            prepare(upper, 1)

    @pl.when(jnp.logical_not(solver))
    def _():
        got = []
        for i in range(pieces):
            remote(ybuf, bcast.at[i], bsend_sem.at[0], brecv_sem.at[i], (r, t * per)).wait_recv()
            got.append(bcast[i])
        value = product(complex_left(got, nvec), fac_hi[...], fac_lo[...], dot_nt)
        vbuf[...] = value
        v_each(lambda copy: copy.start())
        vrecv[c] = value

    @pl.when(j == 0)
    def _():
        prepare_basis()
        side_work()

    @pl.when(t == 0)
    def _():
        @pl.when(jnp.logical_not(solver))
        def _():
            remote(ybuf, ybuf, ysend_sem.at[0], yrecv_sem.at[0], (r, h)).wait_recv()

        g = v_sum(per, C, ybuf[...])
        send_first(g, lead_hi[...], lead_lo[...])
        xbuf[...] = solve(1, g)

    @pl.when(t > 0)
    def _():
        @pl.when(solver)
        def _():
            xbuf[...] = solve(1, v_sum((t + 1) * per, C, ybuf[...]))

            @pl.when(speaks)
            def _():
                each(0, t * share, lambda rr: b_copy(xbuf, rr).start())

            each(0, t, lambda tt: x_copy(tt).start())
            each(t + 1, C // per, lambda tt: x_copy(tt).start())

        @pl.when(jnp.logical_not(solver))
        def _():
            remote(ybuf, xbuf, xsend_sem.at[0], xrecv_sem.at[0], (r, t * per)).wait_recv()

        send_first(xbuf[...], bas_hi[...], bas_lo[...])

    frecv[r] = fsend[...]

    def f_wait(d):
        q = (r + d) % R
        remote(fsend, frecv.at[q], fsend_sem.at[d], frecv_sem.at[q], (q, c)).wait_recv()

    each(1, R, f_wait)
    first = frecv[0]
    for i in range(1, R):
        first = first + frecv[i]
    ends = product(first, end_hi[...], end_lo[...], dot_nn)
    coefficients[0] = ends[:, :nb]
    coefficients[1] = ends[:, nb:2 * nb]
    projected[0] = xbuf[:nvec] - ends[:, 2 * nb:2 * nb + rows]
    projected[1] = xbuf[nvec:] - ends[:, 2 * nb + rows:]

    each(1, R, lambda d: f_copy(d).wait_send())
    for i in range(steps):
        gram_copy(i).wait_send()

    def parts_sent(sweep):
        for d in range(1, share):
            part_copy(sweep, d).wait_send()

    @pl.when(t == 0)
    def _():
        parts_sent(1)
        for d in range(1, share):
            t_copy(d).wait_send()

    @pl.when(solver)
    def _():
        parts_sent(0)

        @pl.when(speaks)
        def _():
            each((t + 1) * share, R, lambda rr: b_copy(ybuf, rr).wait_send())

        @pl.when(t == 0)
        def _():
            each(1, C // per, lambda tt: y_copy(tt).wait_send())

        @pl.when(t > 0)
        def _():
            parts_sent(1)

            @pl.when(speaks)
            def _():
                each(0, t * share, lambda rr: b_copy(xbuf, rr).wait_send())

            each(0, t, lambda tt: x_copy(tt).wait_send())
            each(t + 1, C // per, lambda tt: x_copy(tt).wait_send())

    @pl.when(jnp.logical_not(solver))
    def _():
        v_each(lambda copy: copy.wait_send())


def local(R, C, factor, lower, upper, krylov, basis):
    tile, rows = lower.shape[1], lower.shape[2]
    width = factor.shape[2]
    nvec, nb = krylov.shape[1], basis.shape[1]
    share, per, pieces = tile // rows, tile // width, width // rows
    steps = R.bit_length() - 1
    dma = pltpu.SemaphoreType.DMA
    vmem = pl.BlockSpec(memory_space=pltpu.VMEM)
    block = (2 * nvec, rows)
    projected, turned = pl.pallas_call(
        functools.partial(kernel, R, C),
        out_shape=(
            jax.ShapeDtypeStruct(krylov.shape, F32),
            jax.ShapeDtypeStruct((2, nvec, nb), F32),
        ),
        in_specs=[vmem] * 5,
        out_specs=(vmem, vmem),
        scratch_shapes=[
            pltpu.VMEM((2, tile, 2 * rows), BF16),
            pltpu.VMEM((2, tile, 2 * rows), BF16),
            pltpu.VMEM((rows, 2 * width), BF16),
            pltpu.VMEM((rows, 2 * width), BF16),
            pltpu.VMEM((2 * nb, 2 * rows), BF16),
            pltpu.VMEM((2 * nb, 2 * rows), BF16),
            pltpu.VMEM((2 * nb, 2 * nb + 2 * rows), BF16),
            pltpu.VMEM((2 * nb, 2 * nb + 2 * rows), BF16),
            pltpu.VMEM((2 * nb, 2 * rows), BF16),
            pltpu.VMEM((2 * nb, 2 * rows), BF16),
            pltpu.VMEM((share, 2, nb, rows), F32),
            pltpu.VMEM((2, share) + block, F32),
            pltpu.VMEM((2, share) + block, F32),
            pltpu.VMEM(block, F32),
            pltpu.VMEM(block, F32),
            pltpu.VMEM((pieces,) + block, F32),
            pltpu.VMEM(block, F32),
            pltpu.VMEM((C,) + block, F32),
            pltpu.VMEM((nvec, 2 * nb), F32),
            pltpu.VMEM((R, nvec, 2 * nb), F32),
            pltpu.VMEM((steps + 1, nb, 2 * nb), F32),
            pltpu.VMEM((steps, nb, 2 * nb), F32),
            dma((2, share)),
            dma((2, share)),
            dma((R,)),
            dma((pieces,)),
            dma((C,)),
            dma((C,)),
            dma((C // per,)),
            dma((1,)),
            dma((R,)),
            dma((R,)),
            dma((steps,)),
            dma((steps,)),
            dma((share,)),
            dma((share,)),
            dma((C // per,)),
            dma((1,)),
        ],
        compiler_params=pltpu.CompilerParams(collective_id=0, has_side_effects=True),
        name="krylov_step",
    )(factor, lower, upper, krylov, basis)
    return projected, turned.transpose(0, 2, 1)


def solution(mesh):
    in_specs = (
        P(None, "row", "col"),
        P(None, None, "row"),
        P(None, None, "row"),
        P(None, None, "row"),
        P(None, None, "row"),
    )
    out_specs = (P(None, None, "row"), P())
    body = functools.partial(local, mesh.shape["row"], mesh.shape["col"])
    return jax.shard_map(body, mesh=mesh, in_specs=in_specs, out_specs=out_specs, check_vma=False)
```

```python
import functools

import jax
import jax.numpy as jnp
from jax import lax
from jax.experimental import pallas as pl
from jax.experimental.pallas import tpu as pltpu
from jax.sharding import PartitionSpec as P

MESH = pl.DeviceIdType.MESH
F32 = jnp.float32
BF16 = jnp.bfloat16


def split(value):
    high = value.astype(BF16)
    low = (value - high.astype(F32)).astype(BF16)
    return high, low


def dot_nt(left, right):
    return lax.dot_general(left, right, (((1,), (1,)), ((), ())), preferred_element_type=F32)


def dot_nn(left, right):
    return lax.dot_general(left, right, (((1,), (0,)), ((), ())), preferred_element_type=F32)


def product(left, high, low, dot):
    rows = left.shape[0]
    left_high, left_low = split(left)
    both = dot(jnp.concatenate([left_high, left_low], 0), high)
    return both[:rows] + (both[rows:] + dot(left_high, low))


def complex_left(pieces, nvec):
    re = [x[:nvec] for x in pieces]
    im = [x[nvec:] for x in pieces]
    top = jnp.concatenate(re + [-x for x in im], 1)
    bottom = jnp.concatenate(im + re, 1)
    return jnp.concatenate([top, bottom], 0)


def kernel(
    R, C, factor, lower, upper, krylov, basis, projected, coefficients,
    inv_hi, inv_lo, fac_hi, fac_lo, bas_hi, bas_lo,
    end_hi, end_lo, lead_hi, lead_lo, gather, both_hi, both_lo, slab,
    psend, precv, ybuf, xbuf, bcast, vbuf, vrecv, fsend, frecv, gacc, grecv,
    psend_sem, precv_sem, bsend_sem, brecv_sem, vsend_sem, vrecv_sem, xsend_sem, xrecv_sem,
    fsend_sem, frecv_sem, gsend_sem, grecv_sem, tsend_sem, trecv_sem, ysend_sem, yrecv_sem,
    usend_sem, urecv_sem, zsend_sem,
):
    tile, rows = lower.shape[1], lower.shape[2]
    width = factor.shape[2]
    nvec = krylov.shape[1]
    nb = basis.shape[1]
    share = tile // rows
    per = tile // width
    pieces = width // rows
    steps = R.bit_length() - 1
    r = lax.axis_index("row")
    c = lax.axis_index("col")
    t, p = r // share, r % share
    j, h = c // per, c % per
    solver = j == t
    last = jnp.logical_and(solver, t == C // per - 1)

    barrier = pltpu.get_barrier_semaphore()

    def greet_row(i, carry):
        pl.semaphore_signal(barrier, inc=1, device_id=((r + 1 + i) % R, c), device_id_type=MESH)
        return carry

    def greet_col(i, carry):
        pl.semaphore_signal(barrier, inc=1, device_id=(r, (c + 1 + i) % C), device_id_type=MESH)
        return carry

    lax.fori_loop(0, R - 1, greet_row, 0)
    lax.fori_loop(0, C - 1, greet_col, 0)

    def prepare(ref, slot):
        high, low = split(jnp.concatenate([ref[0], ref[1]], 1))
        inv_hi[slot] = high
        inv_lo[slot] = low

    @pl.when(solver)
    def _():
        prepare(lower, 0)

    @pl.when(jnp.logical_not(solver))
    def _():
        high, low = split(jnp.concatenate([factor[0], factor[1]], 1))
        fac_hi[...] = high
        fac_lo[...] = low

    def prepare_basis():
        top = jnp.concatenate([basis[0], basis[1]], 1)
        bottom = jnp.concatenate([-basis[1], basis[0]], 1)
        high, low = split(jnp.concatenate([top, bottom], 0))
        bas_hi[...] = high
        bas_lo[...] = low
        gacc[0] = product(top, high, low, dot_nt)

    def remote(src, dst, send, recv, dest):
        return pltpu.make_async_remote_copy(
            src_ref=src, dst_ref=dst, send_sem=send, recv_sem=recv, device_id=dest, device_id_type=MESH
        )

    def each(first_index, last_index, act):
        def body(i, carry):
            act(i)
            return carry

        lax.fori_loop(first_index, last_index, body, 0)

    def gram_copy(i):
        other = r + (1 << i) * (1 - 2 * ((r // (1 << i)) % 2))
        return remote(gacc.at[i], grecv.at[i], gsend_sem.at[i], grecv_sem.at[i], (other, c))

    def gram_all():
        for i in range(steps):
            copy = gram_copy(i)
            copy.start()
            copy.wait_recv()
            gacc[i + 1] = gacc[i] + grecv[i]
        top = gacc[steps]
        gram = jnp.concatenate([top, jnp.concatenate([-top[:, nb:], top[:, :nb]], 1)], 0)
        row_id = lax.broadcasted_iota(jnp.int32, gram.shape, 0)
        col_id = lax.broadcasted_iota(jnp.int32, gram.shape, 1)
        twice = jnp.where(row_id == col_id, 2.0, 0.0) - gram
        spread = product(twice, bas_hi[...], bas_lo[...], dot_nn)
        high, low = split(jnp.concatenate([twice, spread], 1))
        end_hi[...] = high
        end_lo[...] = low

    def t_copy(d):
        q = (p + d) % share
        return remote(basis, gather.at[p], tsend_sem.at[d], trecv_sem.at[p], (t * share + q, c))

    def lead_send():
        for d in range(1, share):
            t_copy(d).start()
        gather[p] = basis[...]

    def lead_all():
        for d in range(1, share):
            q = (p + d) % share
            remote(basis, gather.at[q], tsend_sem.at[d], trecv_sem.at[q], (t * share + q, c)).wait_recv()
        left = jnp.concatenate(
            [jnp.concatenate([gather[q, i] for q in range(share)], 1) for i in range(2)], 0
        )
        out = product(left, inv_hi[1], inv_lo[1], dot_nn)
        one = out[:nb, :rows] + out[nb:, rows:]
        two = out[nb:, :rows] - out[:nb, rows:]
        whole = jnp.concatenate([jnp.concatenate([one, two], 1), jnp.concatenate([-two, one], 1)], 0)
        high, low = split(whole)
        lead_hi[...] = high
        lead_lo[...] = low

    def u_copy(d):
        q = (p + d) % share
        source = upper.at[:, pl.ds(pl.multiple_of(h * width, width), width), :]
        return remote(source, slab.at[p], usend_sem.at[d], urecv_sem.at[p], (t * share + q, c))

    def both_all():
        for d in range(1, share):
            q = (p + d) % share
            remote(slab.at[p], slab.at[q], usend_sem.at[d], urecv_sem.at[q], (t * share + q, c)).wait_recv()
        slab[p] = upper[:, pl.ds(pl.multiple_of(h * width, width), width), :]
        for i in range(pieces):
            left = jnp.concatenate(
                [
                    jnp.concatenate([slab[q, k, i * rows:(i + 1) * rows, :] for q in range(share)], 1)
                    for k in range(2)
                ],
                0,
            )
            out = product(left, inv_hi[0], inv_lo[0], dot_nn)
            re = out[:rows, :rows] - out[rows:, rows:]
            im = out[:rows, rows:] + out[rows:, :rows]
            high, low = split(jnp.concatenate([re, im], 1))
            both_hi[i * rows:(i + 1) * rows, :] = high
            both_lo[i * rows:(i + 1) * rows, :] = low

    def side_work():
        @pl.when(t == 0)
        def _():
            lead_send()

        gram_all()

        @pl.when(t == 0)
        def _():
            lead_all()

    def part_copy(sweep, d):
        q = (p + d) % share
        return remote(
            psend.at[sweep, q], precv.at[sweep, p], psend_sem.at[sweep, q], precv_sem.at[sweep, p], (t * share + q, c)
        )

    def part_arrival(sweep, d):
        q = (p + d) % share
        return remote(
            psend.at[sweep, q], precv.at[sweep, q], psend_sem.at[sweep, q], precv_sem.at[sweep, q], (t * share + q, c)
        ), q

    def v_copy(cc):
        return remote(vbuf, vrecv.at[c], vsend_sem.at[cc], vrecv_sem.at[c], (r, cc))

    def v_each(act):
        @pl.when(t > 0)
        def _():
            for hh in range(per):
                act(v_copy(t * per + hh))

        @pl.when(t == 0)
        def _():
            each(1, C, lambda d: act(v_copy((c + d) % C)))

    def v_sum(first_col, last_col, value):
        def body(cc, total):
            @pl.when(cc != c)
            def _():
                remote(vbuf, vrecv.at[cc], vsend_sem.at[0], vrecv_sem.at[cc], (r, cc)).wait_recv()

            return total - vrecv[cc]

        return lax.fori_loop(first_col, last_col, body, value)

    def f_copy(d):
        return remote(fsend, frecv.at[r], fsend_sem.at[d], frecv_sem.at[r], ((r + d) % R, c))

    def send_first(value, high, low):
        wide_value = jnp.concatenate([value[:nvec], value[nvec:]], 1)
        fsend[...] = product(wide_value, high, low, dot_nt)
        each(1, R, lambda d: f_copy(d).start())

    def solve(sweep, g):
        out = product(complex_left([g], nvec), inv_hi[sweep], inv_lo[sweep], dot_nt)
        for q in range(share):
            psend[sweep, q] = out[:, q * rows:(q + 1) * rows]
        for d in range(1, share):
            part_copy(sweep, d).start()
        total = psend[sweep, p]
        for d in range(1, share):
            arrival, q = part_arrival(sweep, d)
            arrival.wait_recv()
            total = total + precv[sweep, q]
        return total

    def w_copy(i):
        q = h * pieces + i
        return remote(
            psend.at[0, q], precv.at[0, p], psend_sem.at[0, q], precv_sem.at[0, p], (t * share + q, c)
        )

    def w_each(act):
        for i in range(pieces):

            @pl.when(h * pieces + i != p)
            def _(i=i):
                act(w_copy(i))

    def w_solve(g):
        out = product(complex_left([g], nvec), both_hi[...], both_lo[...], dot_nt)
        for i in range(pieces):
            psend[0, h * pieces + i] = out[:, i * rows:(i + 1) * rows]
        w_each(lambda copy: copy.start())

    def b_copy(buf, rr):
        return remote(buf, bcast.at[p % pieces], bsend_sem.at[rr], brecv_sem.at[p % pieces], (rr, c))

    def x_copy(tt):
        cc = tt * per + h
        return remote(xbuf, xbuf, xsend_sem.at[tt], xrecv_sem.at[0], (r, cc))

    def z_copy(d):
        return remote(xbuf, xbuf, zsend_sem.at[d], xrecv_sem.at[0], (r, (c + d) % C))

    def y_copy(tt):
        return remote(ybuf, ybuf, ysend_sem.at[tt], yrecv_sem.at[0], (r, tt * per + h))

    speaks = p // pieces == h

    @pl.when(jnp.logical_and(solver != (t == 0), jnp.logical_not(last)))
    def _():
        prepare(upper, 1)

    @pl.when(j > 0)
    def _():
        prepare_basis()

    pl.semaphore_wait(barrier, R - 1 + C - 1)

    @pl.when(last)
    def _():
        for d in range(1, share):
            u_copy(d).start()

    @pl.when(j > 0)
    def _():
        side_work()

    @pl.when(last)
    def _():
        both_all()
        b = jnp.concatenate([krylov[0], krylov[1]], 0)
        w_solve(v_sum(0, t * per, b))

        @pl.when(speaks)
        def _():
            total = psend[0, p]
            for d in range(1, share):
                arrival, q = part_arrival(0, d)
                arrival.wait_recv()
                total = total + precv[0, q]
            xbuf[...] = total
            each(0, t * share, lambda rr: b_copy(xbuf, rr).start())
            each(1, C, lambda d: z_copy(d).start())

    @pl.when(jnp.logical_and(solver, jnp.logical_not(last)))
    def _():
        b = jnp.concatenate([krylov[0], krylov[1]], 0)
        ybuf[...] = solve(0, v_sum(0, t * per, b))

        @pl.when(speaks)
        def _():
            each((t + 1) * share, R, lambda rr: b_copy(ybuf, rr).start())

        @pl.when(t == 0)
        def _():
            each(1, C // per, lambda tt: y_copy(tt).start())
            prepare(upper, 1)

    @pl.when(jnp.logical_not(solver))
    def _():
        got = []
        for i in range(pieces):
            remote(ybuf, bcast.at[i], bsend_sem.at[0], brecv_sem.at[i], (r, t * per)).wait_recv()
            got.append(bcast[i])
        value = product(complex_left(got, nvec), fac_hi[...], fac_lo[...], dot_nt)
        vbuf[...] = value
        v_each(lambda copy: copy.start())
        vrecv[c] = value

    @pl.when(j == 0)
    def _():
        prepare_basis()
        side_work()

    @pl.when(t == 0)
    def _():
        @pl.when(jnp.logical_not(solver))
        def _():
            remote(ybuf, ybuf, ysend_sem.at[0], yrecv_sem.at[0], (r, h)).wait_recv()

        g = v_sum(per, C, ybuf[...])
        send_first(g, lead_hi[...], lead_lo[...])
        xbuf[...] = solve(1, g)

    @pl.when(t > 0)
    def _():
        @pl.when(jnp.logical_and(solver, jnp.logical_not(last)))
        def _():
            xbuf[...] = solve(1, v_sum((t + 1) * per, C, ybuf[...]))

            @pl.when(speaks)
            def _():
                each(0, t * share, lambda rr: b_copy(xbuf, rr).start())

            each(0, t, lambda tt: x_copy(tt).start())
            each(t + 1, C // per, lambda tt: x_copy(tt).start())

        @pl.when(jnp.logical_not(jnp.logical_and(solver, jnp.logical_or(speaks, jnp.logical_not(last)))))
        def _():
            remote(ybuf, xbuf, xsend_sem.at[0], xrecv_sem.at[0], (r, t * per)).wait_recv()

        send_first(xbuf[...], bas_hi[...], bas_lo[...])

    frecv[r] = fsend[...]

    def f_wait(d):
        q = (r + d) % R
        remote(fsend, frecv.at[q], fsend_sem.at[d], frecv_sem.at[q], (q, c)).wait_recv()

    each(1, R, f_wait)
    first = frecv[0]
    for i in range(1, R):
        first = first + frecv[i]
    ends = product(first, end_hi[...], end_lo[...], dot_nn)
    coefficients[0] = ends[:, :nb]
    coefficients[1] = ends[:, nb:2 * nb]
    projected[0] = xbuf[:nvec] - ends[:, 2 * nb:2 * nb + rows]
    projected[1] = xbuf[nvec:] - ends[:, 2 * nb + rows:]

    each(1, R, lambda d: f_copy(d).wait_send())
    for i in range(steps):
        gram_copy(i).wait_send()

    def parts_sent(sweep):
        for d in range(1, share):
            part_copy(sweep, d).wait_send()

    @pl.when(t == 0)
    def _():
        parts_sent(1)
        for d in range(1, share):
            t_copy(d).wait_send()

    @pl.when(last)
    def _():
        for d in range(1, share):
            u_copy(d).wait_send()
        w_each(lambda copy: copy.wait_send())

        @pl.when(speaks)
        def _():
            each(0, t * share, lambda rr: b_copy(xbuf, rr).wait_send())
            each(1, C, lambda d: z_copy(d).wait_send())

    @pl.when(jnp.logical_and(solver, jnp.logical_not(last)))
    def _():
        parts_sent(0)

        @pl.when(speaks)
        def _():
            each((t + 1) * share, R, lambda rr: b_copy(ybuf, rr).wait_send())

        @pl.when(t == 0)
        def _():
            each(1, C // per, lambda tt: y_copy(tt).wait_send())

        @pl.when(t > 0)
        def _():
            parts_sent(1)

            @pl.when(speaks)
            def _():
                each(0, t * share, lambda rr: b_copy(xbuf, rr).wait_send())

            each(0, t, lambda tt: x_copy(tt).wait_send())
            each(t + 1, C // per, lambda tt: x_copy(tt).wait_send())

    @pl.when(jnp.logical_not(solver))
    def _():
        v_each(lambda copy: copy.wait_send())


def local(R, C, factor, lower, upper, krylov, basis):
    tile, rows = lower.shape[1], lower.shape[2]
    width = factor.shape[2]
    nvec, nb = krylov.shape[1], basis.shape[1]
    share, per, pieces = tile // rows, tile // width, width // rows
    steps = R.bit_length() - 1
    dma = pltpu.SemaphoreType.DMA
    vmem = pl.BlockSpec(memory_space=pltpu.VMEM)
    block = (2 * nvec, rows)
    projected, turned = pl.pallas_call(
        functools.partial(kernel, R, C),
        out_shape=(
            jax.ShapeDtypeStruct(krylov.shape, F32),
            jax.ShapeDtypeStruct((2, nvec, nb), F32),
        ),
        in_specs=[vmem] * 5,
        out_specs=(vmem, vmem),
        scratch_shapes=[
            pltpu.VMEM((2, tile, 2 * rows), BF16),
            pltpu.VMEM((2, tile, 2 * rows), BF16),
            pltpu.VMEM((rows, 2 * width), BF16),
            pltpu.VMEM((rows, 2 * width), BF16),
            pltpu.VMEM((2 * nb, 2 * rows), BF16),
            pltpu.VMEM((2 * nb, 2 * rows), BF16),
            pltpu.VMEM((2 * nb, 2 * nb + 2 * rows), BF16),
            pltpu.VMEM((2 * nb, 2 * nb + 2 * rows), BF16),
            pltpu.VMEM((2 * nb, 2 * rows), BF16),
            pltpu.VMEM((2 * nb, 2 * rows), BF16),
            pltpu.VMEM((share, 2, nb, rows), F32),
            pltpu.VMEM((width, 2 * rows), BF16),
            pltpu.VMEM((width, 2 * rows), BF16),
            pltpu.VMEM((share, 2, width, rows), F32),
            pltpu.VMEM((2, share) + block, F32),
            pltpu.VMEM((2, share) + block, F32),
            pltpu.VMEM(block, F32),
            pltpu.VMEM(block, F32),
            pltpu.VMEM((pieces,) + block, F32),
            pltpu.VMEM(block, F32),
            pltpu.VMEM((C,) + block, F32),
            pltpu.VMEM((nvec, 2 * nb), F32),
            pltpu.VMEM((R, nvec, 2 * nb), F32),
            pltpu.VMEM((steps + 1, nb, 2 * nb), F32),
            pltpu.VMEM((steps, nb, 2 * nb), F32),
            dma((2, share)),
            dma((2, share)),
            dma((R,)),
            dma((pieces,)),
            dma((C,)),
            dma((C,)),
            dma((C // per,)),
            dma((1,)),
            dma((R,)),
            dma((R,)),
            dma((steps,)),
            dma((steps,)),
            dma((share,)),
            dma((share,)),
            dma((C // per,)),
            dma((1,)),
            dma((share,)),
            dma((share,)),
            dma((C,)),
        ],
        compiler_params=pltpu.CompilerParams(collective_id=0, has_side_effects=True),
        name="krylov_step",
    )(factor, lower, upper, krylov, basis)
    return projected, turned.transpose(0, 2, 1)


def solution(mesh):
    in_specs = (
        P(None, "row", "col"),
        P(None, None, "row"),
        P(None, None, "row"),
        P(None, None, "row"),
        P(None, None, "row"),
    )
    out_specs = (P(None, None, "row"), P())
    body = functools.partial(local, mesh.shape["row"], mesh.shape["col"])
    return jax.shard_map(body, mesh=mesh, in_specs=in_specs, out_specs=out_specs, check_vma=False)
```

```python
import functools

import jax
import jax.numpy as jnp
from jax import lax
from jax.experimental import pallas as pl
from jax.experimental.pallas import tpu as pltpu
from jax.sharding import PartitionSpec as P

MESH = pl.DeviceIdType.MESH
F32 = jnp.float32
BF16 = jnp.bfloat16


def split(value):
    high = value.astype(BF16)
    low = (value - high.astype(F32)).astype(BF16)
    return high, low


def dot_nt(left, right):
    return lax.dot_general(left, right, (((1,), (1,)), ((), ())), preferred_element_type=F32)


def dot_nn(left, right):
    return lax.dot_general(left, right, (((1,), (0,)), ((), ())), preferred_element_type=F32)


def product(left, high, low, dot):
    rows = left.shape[0]
    left_high, left_low = split(left)
    both = dot(jnp.concatenate([left_high, left_low], 0), high)
    return both[:rows] + (both[rows:] + dot(left_high, low))


def complex_left(pieces, nvec):
    re = [x[:nvec] for x in pieces]
    im = [x[nvec:] for x in pieces]
    top = jnp.concatenate(re + [-x for x in im], 1)
    bottom = jnp.concatenate(im + re, 1)
    return jnp.concatenate([top, bottom], 0)


def kernel(
    R, C, factor, lower, upper, krylov, basis, projected, coefficients,
    inv_hi, inv_lo, fac_hi, fac_lo, bas_hi, bas_lo,
    end_hi, end_lo, lead_hi, lead_lo, gather,
    psend, precv, ybuf, xbuf, bcast, vbuf, vrecv, fsend, frecv, gacc, grecv,
    psend_sem, precv_sem, bsend_sem, brecv_sem, vsend_sem, vrecv_sem, xsend_sem, xrecv_sem,
    fsend_sem, frecv_sem, gsend_sem, grecv_sem, tsend_sem, trecv_sem, ysend_sem, yrecv_sem,
):
    tile, rows = lower.shape[1], lower.shape[2]
    width = factor.shape[2]
    nvec = krylov.shape[1]
    nb = basis.shape[1]
    share = tile // rows
    per = tile // width
    pieces = width // rows
    steps = R.bit_length() - 1
    r = lax.axis_index("row")
    c = lax.axis_index("col")
    t, p = r // share, r % share
    j, h = c // per, c % per
    solver = j == t

    barrier = pltpu.get_barrier_semaphore()

    def greet_row(i, carry):
        pl.semaphore_signal(barrier, inc=1, device_id=((r + 1 + i) % R, c), device_id_type=MESH)
        return carry

    def greet_col(i, carry):
        pl.semaphore_signal(barrier, inc=1, device_id=(r, (c + 1 + i) % C), device_id_type=MESH)
        return carry

    lax.fori_loop(0, R - 1, greet_row, 0)
    lax.fori_loop(0, C - 1, greet_col, 0)

    def prepare(ref, slot):
        high, low = split(jnp.concatenate([ref[0], ref[1]], 1))
        inv_hi[slot] = high
        inv_lo[slot] = low

    @pl.when(solver)
    def _():
        prepare(lower, 0)

    @pl.when(jnp.logical_not(solver))
    def _():
        high, low = split(jnp.concatenate([factor[0], factor[1]], 1))
        fac_hi[...] = high
        fac_lo[...] = low

    def prepare_basis():
        top = jnp.concatenate([basis[0], basis[1]], 1)
        bottom = jnp.concatenate([-basis[1], basis[0]], 1)
        high, low = split(jnp.concatenate([top, bottom], 0))
        bas_hi[...] = high
        bas_lo[...] = low
        gacc[0] = product(top, high, low, dot_nt)

    def remote(src, dst, send, recv, dest):
        return pltpu.make_async_remote_copy(
            src_ref=src, dst_ref=dst, send_sem=send, recv_sem=recv, device_id=dest, device_id_type=MESH
        )

    def each(first_index, last_index, act):
        def body(i, carry):
            act(i)
            return carry

        lax.fori_loop(first_index, last_index, body, 0)

    def gram_copy(i):
        other = r + (1 << i) * (1 - 2 * ((r // (1 << i)) % 2))
        return remote(gacc.at[i], grecv.at[i], gsend_sem.at[i], grecv_sem.at[i], (other, c))

    def gram_all():
        for i in range(steps):
            copy = gram_copy(i)
            copy.start()
            copy.wait_recv()
            gacc[i + 1] = gacc[i] + grecv[i]
        top = gacc[steps]
        gram = jnp.concatenate([top, jnp.concatenate([-top[:, nb:], top[:, :nb]], 1)], 0)
        row_id = lax.broadcasted_iota(jnp.int32, gram.shape, 0)
        col_id = lax.broadcasted_iota(jnp.int32, gram.shape, 1)
        twice = jnp.where(row_id == col_id, 2.0, 0.0) - gram
        spread = product(twice, bas_hi[...], bas_lo[...], dot_nn)
        high, low = split(jnp.concatenate([twice, spread], 1))
        end_hi[...] = high
        end_lo[...] = low

    def t_copy(d):
        q = (p + d) % share
        return remote(basis, gather.at[p], tsend_sem.at[d], trecv_sem.at[p], (t * share + q, c))

    def lead_send():
        for d in range(1, share):
            t_copy(d).start()
        gather[p] = basis[...]

    def lead_all():
        for d in range(1, share):
            q = (p + d) % share
            remote(basis, gather.at[q], tsend_sem.at[d], trecv_sem.at[q], (t * share + q, c)).wait_recv()
        left = jnp.concatenate(
            [jnp.concatenate([gather[q, i] for q in range(share)], 1) for i in range(2)], 0
        )
        out = product(left, inv_hi[1], inv_lo[1], dot_nn)
        one = out[:nb, :rows] + out[nb:, rows:]
        two = out[nb:, :rows] - out[:nb, rows:]
        whole = jnp.concatenate([jnp.concatenate([one, two], 1), jnp.concatenate([-two, one], 1)], 0)
        high, low = split(whole)
        lead_hi[...] = high
        lead_lo[...] = low

    def side_work():
        gram_all()

        @pl.when(t == 0)
        def _():
            lead_send()
            lead_all()

    def part_copy(sweep, d):
        q = (p + d) % share
        return remote(
            psend.at[sweep, q], precv.at[sweep, p], psend_sem.at[sweep, q], precv_sem.at[sweep, p], (t * share + q, c)
        )

    def part_arrival(sweep, d):
        q = (p + d) % share
        return remote(
            psend.at[sweep, q], precv.at[sweep, q], psend_sem.at[sweep, q], precv_sem.at[sweep, q], (t * share + q, c)
        ), q

    def v_copy(cc):
        return remote(vbuf, vrecv.at[c], vsend_sem.at[cc], vrecv_sem.at[c], (r, cc))

    def v_each(act):
        @pl.when(t > 0)
        def _():
            for hh in range(per):
                act(v_copy(t * per + hh))

        @pl.when(t == 0)
        def _():
            each(1, C, lambda d: act(v_copy((c + d) % C)))

    def v_sum(first_col, last_col, value):
        def body(cc, total):
            @pl.when(cc != c)
            def _():
                remote(vbuf, vrecv.at[cc], vsend_sem.at[0], vrecv_sem.at[cc], (r, cc)).wait_recv()

            return total - vrecv[cc]

        return lax.fori_loop(first_col, last_col, body, value)

    def f_copy(d):
        return remote(fsend, frecv.at[r], fsend_sem.at[d], frecv_sem.at[r], ((r + d) % R, c))

    def send_first(value, high, low):
        wide_value = jnp.concatenate([value[:nvec], value[nvec:]], 1)
        fsend[...] = product(wide_value, high, low, dot_nt)
        each(1, R, lambda d: f_copy(d).start())

    def multiply(sweep, g):
        out = product(complex_left([g], nvec), inv_hi[sweep], inv_lo[sweep], dot_nt)
        for q in range(share):
            psend[sweep, q] = out[:, q * rows:(q + 1) * rows]

    def solve(sweep, g):
        multiply(sweep, g)
        return exchange(sweep)

    def exchange(sweep):
        for d in range(1, share):
            part_copy(sweep, d).start()
        total = psend[sweep, p]
        for d in range(1, share):
            arrival, q = part_arrival(sweep, d)
            arrival.wait_recv()
            total = total + precv[sweep, q]
        return total

    def b_copy(buf, rr):
        return remote(buf, bcast.at[p % pieces], bsend_sem.at[rr], brecv_sem.at[p % pieces], (rr, c))

    def x_copy(tt):
        cc = tt * per + h
        return remote(xbuf, xbuf, xsend_sem.at[tt], xrecv_sem.at[0], (r, cc))

    def y_copy(tt):
        return remote(ybuf, ybuf, ysend_sem.at[tt], yrecv_sem.at[0], (r, tt * per + h))

    speaks = p // pieces == h

    @pl.when(solver != (t == 0))
    def _():
        prepare(upper, 1)

    @pl.when(j > 0)
    def _():
        prepare_basis()

    @pl.when(jnp.logical_and(solver, t == 0))
    def _():
        multiply(0, jnp.concatenate([krylov[0], krylov[1]], 0))

    pl.semaphore_wait(barrier, R - 1 + C - 1)

    @pl.when(j > 0)
    def _():
        side_work()

    @pl.when(solver)
    def _():
        @pl.when(t > 0)
        def _():
            b = jnp.concatenate([krylov[0], krylov[1]], 0)
            multiply(0, v_sum(0, t * per, b))

        ybuf[...] = exchange(0)

        @pl.when(speaks)
        def _():
            each((t + 1) * share, R, lambda rr: b_copy(ybuf, rr).start())

        @pl.when(t == 0)
        def _():
            each(1, C // per, lambda tt: y_copy(tt).start())
            prepare(upper, 1)

    @pl.when(jnp.logical_not(solver))
    def _():
        got = []
        for i in range(pieces):
            remote(ybuf, bcast.at[i], bsend_sem.at[0], brecv_sem.at[i], (r, t * per)).wait_recv()
            got.append(bcast[i])
        value = product(complex_left(got, nvec), fac_hi[...], fac_lo[...], dot_nt)
        vbuf[...] = value
        v_each(lambda copy: copy.start())
        vrecv[c] = value

    @pl.when(j == 0)
    def _():
        prepare_basis()
        side_work()

    @pl.when(t == 0)
    def _():
        @pl.when(jnp.logical_not(solver))
        def _():
            remote(ybuf, ybuf, ysend_sem.at[0], yrecv_sem.at[0], (r, h)).wait_recv()

        g = v_sum(per, C, ybuf[...])
        send_first(g, lead_hi[...], lead_lo[...])
        xbuf[...] = solve(1, g)

    @pl.when(t > 0)
    def _():
        @pl.when(solver)
        def _():
            xbuf[...] = solve(1, v_sum((t + 1) * per, C, ybuf[...]))

            @pl.when(speaks)
            def _():
                each(0, t * share, lambda rr: b_copy(xbuf, rr).start())

            each(0, t, lambda tt: x_copy(tt).start())
            each(t + 1, C // per, lambda tt: x_copy(tt).start())

        @pl.when(jnp.logical_not(solver))
        def _():
            remote(ybuf, xbuf, xsend_sem.at[0], xrecv_sem.at[0], (r, t * per)).wait_recv()

        send_first(xbuf[...], bas_hi[...], bas_lo[...])

    frecv[r] = fsend[...]

    def f_wait(d):
        q = (r + d) % R
        remote(fsend, frecv.at[q], fsend_sem.at[d], frecv_sem.at[q], (q, c)).wait_recv()

    each(1, R, f_wait)
    first = frecv[0]
    for i in range(1, R):
        first = first + frecv[i]
    ends = product(first, end_hi[...], end_lo[...], dot_nn)
    coefficients[0] = ends[:, :nb]
    coefficients[1] = ends[:, nb:2 * nb]
    projected[0] = xbuf[:nvec] - ends[:, 2 * nb:2 * nb + rows]
    projected[1] = xbuf[nvec:] - ends[:, 2 * nb + rows:]

    each(1, R, lambda d: f_copy(d).wait_send())
    for i in range(steps):
        gram_copy(i).wait_send()

    def parts_sent(sweep):
        for d in range(1, share):
            part_copy(sweep, d).wait_send()

    @pl.when(t == 0)
    def _():
        parts_sent(1)
        for d in range(1, share):
            t_copy(d).wait_send()

    @pl.when(solver)
    def _():
        parts_sent(0)

        @pl.when(speaks)
        def _():
            each((t + 1) * share, R, lambda rr: b_copy(ybuf, rr).wait_send())

        @pl.when(t == 0)
        def _():
            each(1, C // per, lambda tt: y_copy(tt).wait_send())

        @pl.when(t > 0)
        def _():
            parts_sent(1)

            @pl.when(speaks)
            def _():
                each(0, t * share, lambda rr: b_copy(xbuf, rr).wait_send())

            each(0, t, lambda tt: x_copy(tt).wait_send())
            each(t + 1, C // per, lambda tt: x_copy(tt).wait_send())

    @pl.when(jnp.logical_not(solver))
    def _():
        v_each(lambda copy: copy.wait_send())


def finish(projected, turned, projected_out, turned_out):
    projected_out[...] = projected[...]
    turned_out[...] = turned[...]


def local(R, C, factor, lower, upper, krylov, basis):
    tile, rows = lower.shape[1], lower.shape[2]
    width = factor.shape[2]
    nvec, nb = krylov.shape[1], basis.shape[1]
    share, per, pieces = tile // rows, tile // width, width // rows
    steps = R.bit_length() - 1
    dma = pltpu.SemaphoreType.DMA
    vmem = pl.BlockSpec(memory_space=pltpu.VMEM)
    block = (2 * nvec, rows)
    projected, turned = pl.pallas_call(
        functools.partial(kernel, R, C),
        out_shape=(
            jax.ShapeDtypeStruct(krylov.shape, F32),
            jax.ShapeDtypeStruct((2, nvec, nb), F32),
        ),
        in_specs=[vmem] * 5,
        out_specs=(vmem, vmem),
        scratch_shapes=[
            pltpu.VMEM((2, tile, 2 * rows), BF16),
            pltpu.VMEM((2, tile, 2 * rows), BF16),
            pltpu.VMEM((rows, 2 * width), BF16),
            pltpu.VMEM((rows, 2 * width), BF16),
            pltpu.VMEM((2 * nb, 2 * rows), BF16),
            pltpu.VMEM((2 * nb, 2 * rows), BF16),
            pltpu.VMEM((2 * nb, 2 * nb + 2 * rows), BF16),
            pltpu.VMEM((2 * nb, 2 * nb + 2 * rows), BF16),
            pltpu.VMEM((2 * nb, 2 * rows), BF16),
            pltpu.VMEM((2 * nb, 2 * rows), BF16),
            pltpu.VMEM((share, 2, nb, rows), F32),
            pltpu.VMEM((2, share) + block, F32),
            pltpu.VMEM((2, share) + block, F32),
            pltpu.VMEM(block, F32),
            pltpu.VMEM(block, F32),
            pltpu.VMEM((pieces,) + block, F32),
            pltpu.VMEM(block, F32),
            pltpu.VMEM((C,) + block, F32),
            pltpu.VMEM((nvec, 2 * nb), F32),
            pltpu.VMEM((R, nvec, 2 * nb), F32),
            pltpu.VMEM((steps + 1, nb, 2 * nb), F32),
            pltpu.VMEM((steps, nb, 2 * nb), F32),
            dma((2, share)),
            dma((2, share)),
            dma((R,)),
            dma((pieces,)),
            dma((C,)),
            dma((C,)),
            dma((C // per,)),
            dma((1,)),
            dma((R,)),
            dma((R,)),
            dma((steps,)),
            dma((steps,)),
            dma((share,)),
            dma((share,)),
            dma((C // per,)),
            dma((1,)),
        ],
        compiler_params=pltpu.CompilerParams(collective_id=0, has_side_effects=True),
        name="krylov_step",
    )(factor, lower, upper, krylov, basis)
    projected, turned = pl.pallas_call(
        finish,
        out_shape=(jax.ShapeDtypeStruct(projected.shape, F32), jax.ShapeDtypeStruct(turned.shape, F32)),
        in_specs=[vmem] * 2,
        out_specs=(vmem, vmem),
        name="finish",
    )(projected, turned)
    return projected, turned.transpose(0, 2, 1)


def solution(mesh):
    in_specs = (
        P(None, "row", "col"),
        P(None, None, "row"),
        P(None, None, "row"),
        P(None, None, "row"),
        P(None, None, "row"),
    )
    out_specs = (P(None, None, "row"), P())
    body = functools.partial(local, mesh.shape["row"], mesh.shape["col"])
    return jax.shard_map(body, mesh=mesh, in_specs=in_specs, out_specs=out_specs, check_vma=False)
```

```python
import functools

import jax
import jax.numpy as jnp
from jax import lax
from jax.experimental import pallas as pl
from jax.experimental.pallas import tpu as pltpu
from jax.sharding import PartitionSpec as P

MESH = pl.DeviceIdType.MESH
F32 = jnp.float32
BF16 = jnp.bfloat16


def split(value):
    high = value.astype(BF16)
    low = (value - high.astype(F32)).astype(BF16)
    return high, low


def dot_nt(left, right):
    return lax.dot_general(left, right, (((1,), (1,)), ((), ())), preferred_element_type=F32)


def dot_nn(left, right):
    return lax.dot_general(left, right, (((1,), (0,)), ((), ())), preferred_element_type=F32)


def product(left, high, low, dot):
    rows = left.shape[0]
    left_high, left_low = split(left)
    both = dot(jnp.concatenate([left_high, left_low], 0), high)
    return both[:rows] + (both[rows:] + dot(left_high, low))


def complex_left(pieces, nvec):
    re = [x[:nvec] for x in pieces]
    im = [x[nvec:] for x in pieces]
    top = jnp.concatenate(re + [-x for x in im], 1)
    bottom = jnp.concatenate(im + re, 1)
    return jnp.concatenate([top, bottom], 0)


def kernel(
    R, C, factor, lower, upper, krylov, basis, projected, coefficients,
    inv_hi, inv_lo, fac_hi, fac_lo, bas_hi, bas_lo,
    end_hi, end_lo, lead_hi, lead_lo, gather,
    psend, precv, ybuf, xbuf, bcast, vbuf, vrecv, fsend, frecv, gacc, grecv,
    psend_sem, precv_sem, bsend_sem, brecv_sem, vsend_sem, vrecv_sem, xsend_sem, xrecv_sem,
    fsend_sem, frecv_sem, gsend_sem, grecv_sem, tsend_sem, trecv_sem, ysend_sem, yrecv_sem,
    ready_sem,
):
    tile, rows = lower.shape[1], lower.shape[2]
    width = factor.shape[2]
    nvec = krylov.shape[1]
    nb = basis.shape[1]
    share = tile // rows
    per = tile // width
    pieces = width // rows
    steps = R.bit_length() - 1
    r = lax.axis_index("row")
    c = lax.axis_index("col")
    t, p = r // share, r % share
    j, h = c // per, c % per
    solver = j == t

    barrier = pltpu.get_barrier_semaphore()

    def greet_mate(i, carry):
        pl.semaphore_signal(barrier, inc=1, device_id=(t * share + (p + 1 + i) % share, c), device_id_type=MESH)
        return carry

    def greet_tile(i, carry):
        pl.semaphore_signal(barrier, inc=1, device_id=((r + (1 + i) * share) % R, c), device_id_type=MESH)
        return carry

    def greet_col(i, carry):
        pl.semaphore_signal(barrier, inc=1, device_id=(r, (c + 1 + i) % C), device_id_type=MESH)
        return carry

    lax.fori_loop(0, share - 1, greet_mate, 0)
    lax.fori_loop(0, R // share - 1, greet_tile, 0)
    lax.fori_loop(0, C - 1, greet_col, 0)

    def prepare(ref, slot):
        high, low = split(jnp.concatenate([ref[0], ref[1]], 1))
        inv_hi[slot] = high
        inv_lo[slot] = low

    @pl.when(solver)
    def _():
        prepare(lower, 0)

    @pl.when(jnp.logical_not(solver))
    def _():
        high, low = split(jnp.concatenate([factor[0], factor[1]], 1))
        fac_hi[...] = high
        fac_lo[...] = low

    def prepare_basis():
        top = jnp.concatenate([basis[0], basis[1]], 1)
        bottom = jnp.concatenate([-basis[1], basis[0]], 1)
        high, low = split(jnp.concatenate([top, bottom], 0))
        bas_hi[...] = high
        bas_lo[...] = low
        gacc[0] = product(top, high, low, dot_nt)

    def remote(src, dst, send, recv, dest):
        return pltpu.make_async_remote_copy(
            src_ref=src, dst_ref=dst, send_sem=send, recv_sem=recv, device_id=dest, device_id_type=MESH
        )

    def each(first_index, last_index, act):
        def body(i, carry):
            act(i)
            return carry

        lax.fori_loop(first_index, last_index, body, 0)

    def gram_copy(i):
        other = r + (1 << i) * (1 - 2 * ((r // (1 << i)) % 2))
        return remote(gacc.at[i], grecv.at[i], gsend_sem.at[i], grecv_sem.at[i], (other, c))

    def gram_all():
        for i in range(steps):
            copy = gram_copy(i)
            copy.start()
            copy.wait_recv()
            gacc[i + 1] = gacc[i] + grecv[i]
        top = gacc[steps]
        gram = jnp.concatenate([top, jnp.concatenate([-top[:, nb:], top[:, :nb]], 1)], 0)
        row_id = lax.broadcasted_iota(jnp.int32, gram.shape, 0)
        col_id = lax.broadcasted_iota(jnp.int32, gram.shape, 1)
        twice = jnp.where(row_id == col_id, 2.0, 0.0) - gram
        spread = product(twice, bas_hi[...], bas_lo[...], dot_nn)
        high, low = split(jnp.concatenate([twice, spread], 1))
        end_hi[...] = high
        end_lo[...] = low

    def t_copy(d):
        q = (p + d) % share
        return remote(basis, gather.at[p], tsend_sem.at[d], trecv_sem.at[p], (t * share + q, c))

    def lead_send():
        for d in range(1, share):
            t_copy(d).start()
        gather[p] = basis[...]

    def lead_all():
        for d in range(1, share):
            q = (p + d) % share
            remote(basis, gather.at[q], tsend_sem.at[d], trecv_sem.at[q], (t * share + q, c)).wait_recv()
        left = jnp.concatenate(
            [jnp.concatenate([gather[q, i] for q in range(share)], 1) for i in range(2)], 0
        )
        out = product(left, inv_hi[1], inv_lo[1], dot_nn)
        one = out[:nb, :rows] + out[nb:, rows:]
        two = out[nb:, :rows] - out[:nb, rows:]
        whole = jnp.concatenate([jnp.concatenate([one, two], 1), jnp.concatenate([-two, one], 1)], 0)
        high, low = split(whole)
        lead_hi[...] = high
        lead_lo[...] = low

    def side_work():
        gram_all()

        @pl.when(t == 0)
        def _():
            lead_send()
            lead_all()

    def part_copy(sweep, d):
        q = (p + d) % share
        return remote(
            psend.at[sweep, q], precv.at[sweep, p], psend_sem.at[sweep, q], precv_sem.at[sweep, p], (t * share + q, c)
        )

    def part_arrival(sweep, d):
        q = (p + d) % share
        return remote(
            psend.at[sweep, q], precv.at[sweep, q], psend_sem.at[sweep, q], precv_sem.at[sweep, q], (t * share + q, c)
        ), q

    def v_copy(cc):
        return remote(vbuf, vrecv.at[c], vsend_sem.at[cc], vrecv_sem.at[c], (r, cc))

    def v_each(act):
        @pl.when(t > 0)
        def _():
            for hh in range(per):
                act(v_copy(t * per + hh))

        @pl.when(t == 0)
        def _():
            each(1, C, lambda d: act(v_copy((c + d) % C)))

    def v_sum(first_col, last_col, value):
        def body(cc, total):
            @pl.when(cc != c)
            def _():
                remote(vbuf, vrecv.at[cc], vsend_sem.at[0], vrecv_sem.at[cc], (r, cc)).wait_recv()

            return total - vrecv[cc]

        return lax.fori_loop(first_col, last_col, body, value)

    def f_copy(d):
        return remote(fsend, frecv.at[r], fsend_sem.at[d], frecv_sem.at[r], ((r + d) % R, c))

    def send_first(value, high, low):
        wide_value = jnp.concatenate([value[:nvec], value[nvec:]], 1)
        fsend[...] = product(wide_value, high, low, dot_nt)
        each(1, R, lambda d: f_copy(d).start())

    def multiply(sweep, g):
        out = product(complex_left([g], nvec), inv_hi[sweep], inv_lo[sweep], dot_nt)
        for q in range(share):
            psend[sweep, q] = out[:, q * rows:(q + 1) * rows]

    def solve(sweep, g):
        multiply(sweep, g)
        return exchange(sweep)

    def exchange(sweep):
        for d in range(1, share):
            part_copy(sweep, d).start()
        total = psend[sweep, p]
        for d in range(1, share):
            arrival, q = part_arrival(sweep, d)
            arrival.wait_recv()
            total = total + precv[sweep, q]
        return total

    def b_copy(buf, rr):
        return remote(buf, bcast.at[p % pieces], bsend_sem.at[rr], brecv_sem.at[p % pieces], (rr, c))

    def x_copy(tt):
        cc = tt * per + h
        return remote(xbuf, xbuf, xsend_sem.at[tt], xrecv_sem.at[0], (r, cc))

    def y_copy(tt):
        return remote(ybuf, ybuf, ysend_sem.at[tt], yrecv_sem.at[0], (r, tt * per + h))

    speaks = p // pieces == h

    @pl.when(solver != (t == 0))
    def _():
        prepare(upper, 1)

    @pl.when(j > 0)
    def _():
        prepare_basis()

    @pl.when(jnp.logical_and(solver, t == 0))
    def _():
        multiply(0, jnp.concatenate([krylov[0], krylov[1]], 0))

    pl.semaphore_wait(barrier, share - 1 + R // share - 1 + C - 1)
    for d in range(1, share):
        pl.semaphore_signal(
            ready_sem, inc=1, device_id=(t * share + (p + d) % share, c), device_id_type=MESH
        )

    @pl.when(j > 0)
    def _():
        side_work()

    @pl.when(solver)
    def _():
        @pl.when(t > 0)
        def _():
            b = jnp.concatenate([krylov[0], krylov[1]], 0)
            multiply(0, v_sum(0, t * per, b))

        ybuf[...] = exchange(0)
        pl.semaphore_wait(ready_sem, share - 1)

        @pl.when(speaks)
        def _():
            each((t + 1) * share, R, lambda rr: b_copy(ybuf, rr).start())

        @pl.when(t == 0)
        def _():
            each(1, C // per, lambda tt: y_copy(tt).start())
            prepare(upper, 1)

    @pl.when(jnp.logical_not(solver))
    def _():
        pl.semaphore_wait(ready_sem, share - 1)
        got = []
        for i in range(pieces):
            remote(ybuf, bcast.at[i], bsend_sem.at[0], brecv_sem.at[i], (r, t * per)).wait_recv()
            got.append(bcast[i])
        value = product(complex_left(got, nvec), fac_hi[...], fac_lo[...], dot_nt)
        vbuf[...] = value
        v_each(lambda copy: copy.start())
        vrecv[c] = value

    @pl.when(j == 0)
    def _():
        prepare_basis()
        side_work()

    @pl.when(t == 0)
    def _():
        @pl.when(jnp.logical_not(solver))
        def _():
            remote(ybuf, ybuf, ysend_sem.at[0], yrecv_sem.at[0], (r, h)).wait_recv()

        g = v_sum(per, C, ybuf[...])
        send_first(g, lead_hi[...], lead_lo[...])
        xbuf[...] = solve(1, g)

    @pl.when(t > 0)
    def _():
        @pl.when(solver)
        def _():
            xbuf[...] = solve(1, v_sum((t + 1) * per, C, ybuf[...]))

            @pl.when(speaks)
            def _():
                each(0, t * share, lambda rr: b_copy(xbuf, rr).start())

            each(0, t, lambda tt: x_copy(tt).start())
            each(t + 1, C // per, lambda tt: x_copy(tt).start())

        @pl.when(jnp.logical_not(solver))
        def _():
            remote(ybuf, xbuf, xsend_sem.at[0], xrecv_sem.at[0], (r, t * per)).wait_recv()

        send_first(xbuf[...], bas_hi[...], bas_lo[...])

    frecv[r] = fsend[...]

    def f_wait(d):
        q = (r + d) % R
        remote(fsend, frecv.at[q], fsend_sem.at[d], frecv_sem.at[q], (q, c)).wait_recv()

    each(1, R, f_wait)
    first = frecv[0]
    for i in range(1, R):
        first = first + frecv[i]
    ends = product(first, end_hi[...], end_lo[...], dot_nn)
    coefficients[0] = ends[:, :nb]
    coefficients[1] = ends[:, nb:2 * nb]
    projected[0] = xbuf[:nvec] - ends[:, 2 * nb:2 * nb + rows]
    projected[1] = xbuf[nvec:] - ends[:, 2 * nb + rows:]

    each(1, R, lambda d: f_copy(d).wait_send())
    for i in range(steps):
        gram_copy(i).wait_send()

    def parts_sent(sweep):
        for d in range(1, share):
            part_copy(sweep, d).wait_send()

    @pl.when(t == 0)
    def _():
        parts_sent(1)
        for d in range(1, share):
            t_copy(d).wait_send()

    @pl.when(solver)
    def _():
        parts_sent(0)

        @pl.when(speaks)
        def _():
            each((t + 1) * share, R, lambda rr: b_copy(ybuf, rr).wait_send())

        @pl.when(t == 0)
        def _():
            each(1, C // per, lambda tt: y_copy(tt).wait_send())

        @pl.when(t > 0)
        def _():
            parts_sent(1)

            @pl.when(speaks)
            def _():
                each(0, t * share, lambda rr: b_copy(xbuf, rr).wait_send())

            each(0, t, lambda tt: x_copy(tt).wait_send())
            each(t + 1, C // per, lambda tt: x_copy(tt).wait_send())

    @pl.when(jnp.logical_not(solver))
    def _():
        v_each(lambda copy: copy.wait_send())


def finish(projected, turned, projected_out, turned_out):
    projected_out[...] = projected[...]
    turned_out[...] = turned[...]


def local(R, C, factor, lower, upper, krylov, basis):
    tile, rows = lower.shape[1], lower.shape[2]
    width = factor.shape[2]
    nvec, nb = krylov.shape[1], basis.shape[1]
    share, per, pieces = tile // rows, tile // width, width // rows
    steps = R.bit_length() - 1
    dma = pltpu.SemaphoreType.DMA
    vmem = pl.BlockSpec(memory_space=pltpu.VMEM)
    block = (2 * nvec, rows)
    projected, turned = pl.pallas_call(
        functools.partial(kernel, R, C),
        out_shape=(
            jax.ShapeDtypeStruct(krylov.shape, F32),
            jax.ShapeDtypeStruct((2, nvec, nb), F32),
        ),
        in_specs=[vmem] * 5,
        out_specs=(vmem, vmem),
        scratch_shapes=[
            pltpu.VMEM((2, tile, 2 * rows), BF16),
            pltpu.VMEM((2, tile, 2 * rows), BF16),
            pltpu.VMEM((rows, 2 * width), BF16),
            pltpu.VMEM((rows, 2 * width), BF16),
            pltpu.VMEM((2 * nb, 2 * rows), BF16),
            pltpu.VMEM((2 * nb, 2 * rows), BF16),
            pltpu.VMEM((2 * nb, 2 * nb + 2 * rows), BF16),
            pltpu.VMEM((2 * nb, 2 * nb + 2 * rows), BF16),
            pltpu.VMEM((2 * nb, 2 * rows), BF16),
            pltpu.VMEM((2 * nb, 2 * rows), BF16),
            pltpu.VMEM((share, 2, nb, rows), F32),
            pltpu.VMEM((2, share) + block, F32),
            pltpu.VMEM((2, share) + block, F32),
            pltpu.VMEM(block, F32),
            pltpu.VMEM(block, F32),
            pltpu.VMEM((pieces,) + block, F32),
            pltpu.VMEM(block, F32),
            pltpu.VMEM((C,) + block, F32),
            pltpu.VMEM((nvec, 2 * nb), F32),
            pltpu.VMEM((R, nvec, 2 * nb), F32),
            pltpu.VMEM((steps + 1, nb, 2 * nb), F32),
            pltpu.VMEM((steps, nb, 2 * nb), F32),
            dma((2, share)),
            dma((2, share)),
            dma((R,)),
            dma((pieces,)),
            dma((C,)),
            dma((C,)),
            dma((C // per,)),
            dma((1,)),
            dma((R,)),
            dma((R,)),
            dma((steps,)),
            dma((steps,)),
            dma((share,)),
            dma((share,)),
            dma((C // per,)),
            dma((1,)),
            pltpu.SemaphoreType.REGULAR,
        ],
        compiler_params=pltpu.CompilerParams(collective_id=0, has_side_effects=True),
        name="krylov_step",
    )(factor, lower, upper, krylov, basis)
    projected, turned = pl.pallas_call(
        finish,
        out_shape=(jax.ShapeDtypeStruct(projected.shape, F32), jax.ShapeDtypeStruct(turned.shape, F32)),
        in_specs=[vmem] * 2,
        out_specs=(vmem, vmem),
        name="finish",
    )(projected, turned)
    return projected, turned.transpose(0, 2, 1)


def solution(mesh):
    in_specs = (
        P(None, "row", "col"),
        P(None, None, "row"),
        P(None, None, "row"),
        P(None, None, "row"),
        P(None, None, "row"),
    )
    out_specs = (P(None, None, "row"), P())
    body = functools.partial(local, mesh.shape["row"], mesh.shape["col"])
    return jax.shard_map(body, mesh=mesh, in_specs=in_specs, out_specs=out_specs, check_vma=False)
```
